256 devices in a mesh: section: 4 (over z_lo), dp: 64 (over x, y, z_hi, core).
Axes of the slice: x: 4, y: 4, z: 8 (z_hi: 2, z_lo: 4; z = z_hi * 4 + z_lo), core: 2. Of those that a mesh axis runs over, the one named last changes fastest.
Arguments:
- section_inputs: bfloat16 [4, 12544, 2048], P('section', 'dp'), may hold values from -16 to 16
- norm_gain: float32 [4, 2048], P('section'), may hold values from 0.25 to 1.75
- query_gain: float32 [4, 2048], P('section'), may hold values from -5 to 5
- key_gain: float32 [4, 2048], P('section'), may hold values from -5 to 5
- output_weight: bfloat16 [4, 2048, 2048], P('section', 'dp'), may hold values from -0.125 to 0.125
- full_sequence_gradient: bfloat16 [256, 196, 2048], P('dp'), may hold values from -6 to 6
- patch_order: int32 [256, 196], P('dp'), may hold values from 0 to 195, each once within a row
Outputs:
- input_grads: bfloat16 [4, 12544, 2048], P('section', 'dp')
- weight_grads: float32 [4, 2048, 2048], P('section', 'dp')
- gain_grads: float32 [4, 3, 2048], P('section')
The draws below stay inside these ranges and needn't reach their ends.
Inputs may be any that keep to these rules, and one draw needn't show every extreme that they name: `patch_order`: each row holds every patch number once; the first 49 are the kept patches.
All inputs are finite; a program needn't handle non-finite values.
Results may differ from the reference program's by a relative error of at most 0.0057.
Values may be sent and summed in bfloat16 or wider, within the bound.
A program may use at most 128 MiB of HBM per device.

```python
import math
import jax
import jax.numpy as jnp
from jax import lax

HEADS = 16
HEAD = 128
D = 2048
KEPT = 49
PATCHES = 196
LAYERS = 4
IMAGES = 256


def gain_levels(key, which):
    base = jax.random.fold_in(key, 71)
    return 1.2 * jax.random.truncated_normal(jax.random.fold_in(base, 5 + which), -4.0, 4.0, (LAYERS, HEADS * HEAD), dtype=jnp.float32)


def draw_query_gain(key, part):
    return gain_levels(key, 0)


def draw_key_gain(key, part):
    return gain_levels(key, 1)


def draw_section_inputs(key, part):
    base = jax.random.fold_in(key, 13)
    shape = (LAYERS, IMAGES, KEPT, HEADS * HEAD)
    values = jax.random.truncated_normal(jax.random.fold_in(base, 3), -6.0, 6.0, shape, dtype=jnp.float32)
    return values.reshape(LAYERS, IMAGES * KEPT, HEADS * HEAD).astype(jnp.bfloat16)


def steps_of(own_key, dims, cuts, low, largest):
    factor_of = 1.0
    for dim, shards_of in cuts:
        heights = jax.random.uniform(jax.random.fold_in(jax.random.fold_in(own_key, 6), dim), (shards_of,), jnp.float32, low / len(cuts), largest / len(cuts))
        factor_of = factor_of * jnp.repeat(jnp.exp(heights), dims[dim] // shards_of).reshape((-1,) + (1,) * (len(dims) - 1 - dim))
    return factor_of


def normal_values(stream_key, shape, width, limit, split=(), kind=jnp.bfloat16):
    entries = jax.random.normal(stream_key, shape, jnp.float32) * width
    if len(split) > 0:
        entries = steps_of(stream_key, shape, split, -0.22, 0.18) * entries
    return jnp.clip(entries, min=-limit, max=limit).astype(kind)


def setup_inputs(seed: int = 0) -> dict:
    arg_keys = jax.random.split(jax.random.key(seed), 8)
    section_inputs = draw_section_inputs(jax.random.fold_in(arg_keys[7], 71), 0)
    norm_gain = jnp.clip(1.0 + 0.15 * jax.random.normal(arg_keys[1], (LAYERS, D), jnp.float32), 0.25, 1.75)
    query_gain = draw_query_gain(jax.random.fold_in(arg_keys[7], 71), 0)
    key_gain = draw_key_gain(jax.random.fold_in(arg_keys[7], 71), 0)
    output_weight = normal_values(arg_keys[4], (LAYERS, D, D), D ** -0.5, 0.125, ((0, 4), (1, 64)))
    full_sequence_gradient = normal_values(arg_keys[5], (IMAGES, PATCHES, D), 1.0, 6.0, ((0, 64),))
    patch_order = jax.vmap(lambda own: jax.random.permutation(own, PATCHES))(jax.random.split(arg_keys[6], IMAGES)).reshape((IMAGES, PATCHES)).astype(jnp.int32)
    return {"section_inputs": section_inputs, "norm_gain": norm_gain, "query_gain": query_gain, "key_gain": key_gain, "output_weight": output_weight, "full_sequence_gradient": full_sequence_gradient, "patch_order": patch_order}


highest = lax.Precision.HIGHEST

def normalize(inputs):
    values = inputs.astype(jnp.float32)
    centred = values - lax.optimization_barrier(jnp.mean(values, axis=-1, keepdims=True))
    variance = lax.optimization_barrier(jnp.mean(centred * centred, axis=-1, keepdims=True))
    inverse = lax.rsqrt(variance + 1e-06)
    return (centred * inverse, inverse)

def attend_forward(normed, gain_row, query_row, key_row, heads):
    row_count, feature_width = normed.shape
    head_width = feature_width // heads
    split_shape = (row_count // KEPT, KEPT, heads, head_width)
    hidden = normed * gain_row
    queries = (hidden * query_row).reshape(split_shape)
    key_rows = (hidden * key_row).reshape(split_shape)
    value_rows = hidden.reshape(split_shape)
    attention_logits = jnp.einsum('bqhd,bkhd->bhqk', queries, key_rows, precision=highest) / math.sqrt(head_width)
    softmaxed = jax.nn.softmax(attention_logits, axis=-1)
    mixed = jnp.einsum('bhqk,bkhd->bqhd', softmaxed, value_rows, precision=highest)
    return (hidden, queries, key_rows, value_rows, softmaxed, mixed.reshape(row_count, feature_width).astype(jnp.bfloat16))

def attend_backward(cotangent, back, normed, inverse, hidden, queries, key_rows, value_rows, softmaxed, gain_row, query_row, key_row):
    row_count, feature_width = back.shape
    head_width = queries.shape[-1]
    back_split = back.reshape(queries.shape)
    soft_grad = jnp.einsum('bqhd,bkhd->bhqk', back_split, value_rows, precision=highest)
    value_grad = jnp.einsum('bhqk,bqhd->bkhd', softmaxed, back_split, precision=highest).reshape(row_count, feature_width)
    score_grad = softmaxed * (soft_grad - lax.optimization_barrier(jnp.sum(soft_grad * softmaxed, axis=-1, keepdims=True))) / math.sqrt(head_width)
    query_grad = jnp.einsum('bhqk,bkhd->bqhd', score_grad, key_rows, precision=highest).reshape(row_count, feature_width)
    key_grad = jnp.einsum('bhqk,bqhd->bkhd', score_grad, queries, precision=highest).reshape(row_count, feature_width)
    hidden_grad = query_grad * query_row + key_grad * key_row + value_grad
    normed_grad = hidden_grad * gain_row
    first_mean = lax.optimization_barrier(jnp.mean(normed_grad, axis=-1, keepdims=True))
    second_mean = lax.optimization_barrier(jnp.mean(normed_grad * normed, axis=-1, keepdims=True))
    input_grad = (cotangent.astype(jnp.float32) + inverse * (normed_grad - first_mean - normed * second_mean)).astype(jnp.bfloat16)
    sums = jnp.stack([lax.optimization_barrier(jnp.sum(hidden_grad * normed, axis=0)), lax.optimization_barrier(jnp.sum(query_grad * hidden, axis=0)), lax.optimization_barrier(jnp.sum(key_grad * hidden, axis=0))])
    return (input_grad, sums)

def reference(section_inputs, norm_gain, query_gain, key_gain, output_weight, full_sequence_gradient, patch_order):
    image_count = patch_order.shape[0]
    feature_width = section_inputs.shape[-1]
    kept = patch_order[:, :KEPT]
    chosen_patches = (kept[:, :, None] == jnp.arange(PATCHES, dtype=jnp.int32)[None, None, :]).astype(jnp.float32)
    upper_bound = jnp.einsum('usn,unj->usj', chosen_patches, full_sequence_gradient.astype(jnp.float32)).reshape(-1, feature_width).astype(jnp.bfloat16)
    cotangent = upper_bound
    gradient_entries, weights_list, gains_list = ([], [], [])
    for layer in range(LAYERS - 1, -1, -1):
        inputs = section_inputs[layer]
        normed, inverse = normalize(inputs)
        hidden, queries, key_rows, value_rows, softmaxed, mixed = attend_forward(normed, norm_gain[layer], query_gain[layer], key_gain[layer], HEADS)
        back = jnp.dot(cotangent, output_weight[layer].T, preferred_element_type=jnp.float32)
        input_grad, sums = attend_backward(cotangent, back, normed, inverse, hidden, queries, key_rows, value_rows, softmaxed, norm_gain[layer], query_gain[layer], key_gain[layer])
        weight_grad = jnp.dot(mixed.T, cotangent, preferred_element_type=jnp.float32) / image_count
        gradient_entries.insert(0, input_grad)
        weights_list.insert(0, weight_grad)
        gains_list.insert(0, sums / image_count)
        cotangent = input_grad
    return (jnp.stack(gradient_entries), jnp.stack(weights_list), jnp.stack(gains_list))
```

```python
import functools
import math

import jax
import jax.numpy as jnp
import numpy as np
from jax import lax
from jax.experimental import pallas as pl
from jax.experimental.pallas import tpu as pltpu
from jax.sharding import PartitionSpec as P


HEADS = 16
KEPT = 49
PATCHES = 196
MICRO = 2


MESH = pl.DeviceIdType.MESH
COLORS = 4
CHUNKS = 64
DIMS = ("x1", "y1", "x2", "y2")
MASKS = {"core": 1, "z": 2, "x1": 16, "x2": 48, "y1": 4, "y2": 12}
PARTNERS = ("core", "x1", "y1", "x2", "y2", "z")


def flip(d, dim):
    if dim == "core":
        return d + 1 - 2 * (d % 2)
    if dim == "z":
        return d + 2 * (1 - 2 * ((d // 2) % 2))
    if dim == "x1":
        return d + 16 * (1 - 2 * ((d // 16) % 2))
    if dim == "x2":
        return d + 16 * (3 - 2 * (d // 16))
    if dim == "y1":
        return d + 4 * (1 - 2 * ((d // 4) % 2))
    return d + 4 * (3 - 2 * ((d // 4) % 4))


def color_dims(color):
    return [DIMS[(color + t) % 4] for t in range(4)]


def relative_masks():
    table = np.zeros((COLORS, CHUNKS), np.int32)
    for color in range(COLORS):
        order = ["core"] + color_dims(color) + ["z"]
        for slot in range(CHUNKS):
            mask = 0
            for bit, dim in enumerate(order):
                if (slot >> (5 - bit)) & 1:
                    mask ^= MASKS[dim]
            table[color, slot] = mask
    return table


def greet(section, me):
    barrier = pltpu.get_barrier_semaphore()
    for dim in PARTNERS:
        pl.semaphore_signal(barrier, inc=1, device_id=(section, flip(me, dim)), device_id_type=MESH)
    pl.semaphore_wait(barrier, len(PARTNERS))


def gather_kernel(w_ref, out_ref, local_sem, z_send, z_recv, d_send, d_recv, c_send, c_recv):
    section = lax.axis_index("section")
    me = lax.axis_index("dp")
    depth, width = w_ref.shape
    cols = width // COLORS
    greet(section, me)

    def rows(chunk):
        return pl.ds(pl.multiple_of(chunk * depth, depth), depth)

    def send(src, dst, s_sem, r_sem, dim):
        pltpu.make_async_remote_copy(
            src_ref=src,
            dst_ref=dst,
            send_sem=s_sem,
            recv_sem=r_sem,
            device_id=(section, flip(me, dim)),
            device_id_type=MESH,
        ).start()

    def view(count, wide):
        return out_ref.at[pl.ds(0, count * depth), pl.ds(0, wide)]

    def drain(count, wide, sem):
        ref = view(count, wide)
        pltpu.make_async_copy(ref, ref, sem).wait()

    local = pltpu.make_async_copy(w_ref, out_ref.at[rows(me)], local_sem)
    local.start()
    send(w_ref, out_ref.at[rows(me)], z_send, z_recv, "z")
    send(w_ref, out_ref.at[rows(me)], c_send.at[0, 0], c_recv.at[0, 0], "core")
    other = flip(me, "z")
    drain(1, width, z_recv)
    send(out_ref.at[rows(other)], out_ref.at[rows(other)], c_send.at[0, 1], c_recv.at[0, 1], "core")
    owned = [[me, other] for _ in range(COLORS)]
    fresh = [[] for _ in range(COLORS)]
    for t in range(4):
        for color in range(COLORS):
            dim = color_dims(color)[t]
            band = pl.ds(color * cols, cols)
            if t > 0:
                drain(len(fresh[color]), cols, d_recv.at[t - 1, color])
            for chunk in owned[color]:
                src = w_ref.at[:, band] if chunk is me else out_ref.at[rows(chunk), band]
                send(src, out_ref.at[rows(chunk), band], d_send.at[t, color], d_recv.at[t, color], dim)
            for chunk in fresh[color]:
                piece = out_ref.at[rows(chunk), band]
                send(piece, piece, c_send.at[t, color], c_recv.at[t, color], "core")
            fresh[color] = [flip(chunk, dim) for chunk in owned[color]]
            owned[color] = owned[color] + fresh[color]
    for color in range(COLORS):
        band = pl.ds(color * cols, cols)
        drain(16, cols, d_recv.at[3, color])
        for chunk in fresh[color]:
            piece = out_ref.at[rows(chunk), band]
            send(piece, piece, c_send.at[4, color], c_recv.at[4, color], "core")
    local.wait()
    drain(1, width, z_send)
    for k in range(2):
        drain(1, width, c_send.at[0, k])
        drain(1, width, c_recv.at[0, k])
    for t in range(4):
        for color in range(COLORS):
            drain(2 << t, cols, d_send.at[t, color])
            drain(2 << t, cols, c_send.at[t + 1, color])
            drain(2 << t, cols, c_recv.at[t + 1, color])


def gather_rows(block):
    depth, width = block.shape
    dma = pltpu.SemaphoreType.DMA
    return pl.pallas_call(
        gather_kernel,
        out_shape=jax.ShapeDtypeStruct((depth * CHUNKS, width), block.dtype),
        in_specs=[pl.BlockSpec(memory_space=pltpu.VMEM)],
        out_specs=pl.BlockSpec(memory_space=pltpu.VMEM),
        scratch_shapes=[dma, dma, dma, dma((4, 4)), dma((4, 4)), dma((5, 4)), dma((5, 4))],
        compiler_params=pltpu.CompilerParams(
            collective_id=0, has_side_effects=True, vmem_limit_bytes=32 * 2**20
        ),
        name="gather_rows",
    )(block)


def half(t):
    return 1024 >> t


def offset(t):
    return 2048 - (2048 >> t)


def reduce_kernel(scale, m_ref, g_ref, s_ref, out_ref, gain_ref, acc, snd, rcv, gs, gr, s_sem, r_sem, gs_sem, gr_sem):
    section = lax.axis_index("section")
    me = lax.axis_index("dp")
    cols = g_ref.shape[1] // COLORS
    tile = 128
    greet(section, me)

    def copy(color, t):
        dim = (["core"] + color_dims(color) + ["z"])[t]
        span = pl.ds(offset(t), half(t))
        return pltpu.make_async_remote_copy(
            src_ref=snd.at[color, span],
            dst_ref=rcv.at[color, span],
            send_sem=s_sem.at[t, color],
            recv_sem=r_sem.at[t, color],
            device_id=(section, flip(me, dim)),
            device_id_type=MESH,
        )

    def gain_copy(t):
        return pltpu.make_async_remote_copy(
            src_ref=gs.at[t],
            dst_ref=gr.at[t],
            send_sem=gs_sem.at[t],
            recv_sem=gr_sem.at[t],
            device_id=(section, flip(me, PARTNERS[t])),
            device_id_type=MESH,
        )

    def tiles(count, body):
        step = min(tile, count)

        def inner(i, carry):
            body(pl.multiple_of(i * step, step), step)
            return carry

        lax.fori_loop(0, count // step, inner, 0)

    def product(color, start, step):
        return lax.dot_general(
            m_ref[color, pl.ds(start, step), :],
            g_ref[:, color * cols : (color + 1) * cols],
            (((1,), (0,)), ((), ())),
            preferred_element_type=jnp.float32,
        )

    gs[0] = s_ref[...]
    for color in range(COLORS):

        def first(start, step, color=color):
            snd[color, pl.ds(start, step), :] = product(color, half(0) + start, step).astype(jnp.bfloat16)

        tiles(half(0), first)
        copy(color, 0).start()
    gain_copy(0).start()
    for color in range(COLORS):

        def own(start, step, color=color):
            acc[color, pl.ds(start, step), :] = product(color, start, step)

        tiles(half(0), own)
    for t in range(1, 6):
        for color in range(COLORS):
            copy(color, t - 1).wait_recv()

            def pass_on(start, step, color=color):
                total = acc[color, pl.ds(half(t) + start, step), :] + rcv[
                    color, pl.ds(offset(t - 1) + half(t) + start, step), :
                ].astype(jnp.float32)
                snd[color, pl.ds(offset(t) + start, step), :] = total.astype(jnp.bfloat16)

            tiles(half(t), pass_on)
            copy(color, t).start()
        gain_copy(t - 1).wait_recv()
        gs[t] = gs[t - 1] + gr[t - 1]
        gain_copy(t).start()
        for color in range(COLORS):

            def keep(start, step, color=color):
                acc[color, pl.ds(start, step), :] += rcv[
                    color, pl.ds(offset(t - 1) + start, step), :
                ].astype(jnp.float32)

            tiles(half(t), keep)
    last = half(5)
    for color in range(COLORS):
        copy(color, 5).wait_recv()
        total = acc[color, 0:last, :] + rcv[color, offset(5) : offset(5) + last, :].astype(jnp.float32)
        out_ref[:, color * cols : (color + 1) * cols] = total * scale
    gain_copy(5).wait_recv()
    gain_ref[...] = (gs[5] + gr[5]) * scale
    for t in range(6):
        gain_copy(t).wait_send()
        for color in range(COLORS):
            copy(color, t).wait_send()


def reduce_rows(ordered, right, sums, scale):
    depth = ordered.shape[1] // CHUNKS
    width = right.shape[1]
    cols = width // COLORS
    dma = pltpu.SemaphoreType.DMA
    total = offset(6)
    vmem = pl.BlockSpec(memory_space=pltpu.VMEM)
    return pl.pallas_call(
        functools.partial(reduce_kernel, scale),
        out_shape=(
            jax.ShapeDtypeStruct((depth, width), jnp.float32),
            jax.ShapeDtypeStruct(sums.shape, jnp.float32),
        ),
        in_specs=[vmem] * 3,
        out_specs=(vmem, vmem),
        scratch_shapes=[
            pltpu.VMEM((COLORS, half(0), cols), jnp.float32),
            pltpu.VMEM((COLORS, total, cols), jnp.bfloat16),
            pltpu.VMEM((COLORS, total, cols), jnp.bfloat16),
            pltpu.VMEM((6,) + sums.shape, jnp.float32),
            pltpu.VMEM((6,) + sums.shape, jnp.float32),
            dma((6, 4)),
            dma((6, 4)),
            dma((6,)),
            dma((6,)),
        ],
        compiler_params=pltpu.CompilerParams(
            collective_id=1, has_side_effects=True, vmem_limit_bytes=48 * 2**20
        ),
        name="reduce_rows",
    )(ordered, right, sums)


def relative_order(mixed):
    rows, width = mixed.shape
    me = lax.axis_index("dp")
    index = jnp.bitwise_xor(jnp.asarray(relative_masks()), me)
    turned = jnp.pad(mixed.T, ((0, 0), (0, 256 - rows))).reshape(CHUNKS, width // CHUNKS, 256)
    return turned[index].reshape(COLORS, width, 256)


highest = lax.Precision.HIGHEST


def from_behind(block, axis, distance):
    devices = range(lax.axis_size(axis))
    route = [(i - distance, i) for i in devices if i - distance in devices]
    return lax.ppermute(block, axis, route)


def normalize(inputs):
    values = inputs.astype(jnp.float32)
    centred = values - jnp.mean(values, axis=-1, keepdims=True)
    variance = jnp.mean(centred * centred, axis=-1, keepdims=True)
    inverse = lax.rsqrt(variance + 1e-06)
    return (centred * inverse, inverse)


def attend_forward(normed, gain_row, query_row, key_row, heads):
    row_count, feature_width = normed.shape
    head_width = feature_width // heads
    split_shape = (row_count // KEPT, KEPT, heads, head_width)
    hidden = normed * gain_row
    queries = (hidden * query_row).reshape(split_shape)
    key_rows = (hidden * key_row).reshape(split_shape)
    value_rows = hidden.reshape(split_shape)
    attention_logits = jnp.einsum(
        "bqhd,bkhd->bhqk", queries, key_rows, precision=highest
    ) / math.sqrt(head_width)
    softmaxed = jax.nn.softmax(attention_logits, axis=-1)
    mixed = jnp.einsum("bhqk,bkhd->bqhd", softmaxed, value_rows, precision=highest)
    return (
        hidden,
        queries,
        key_rows,
        value_rows,
        softmaxed,
        mixed.reshape(row_count, feature_width).astype(jnp.bfloat16),
    )


def attend_backward(
    cotangent,
    back,
    normed,
    inverse,
    hidden,
    queries,
    key_rows,
    value_rows,
    softmaxed,
    gain_row,
    query_row,
    key_row,
):
    row_count, feature_width = back.shape
    head_width = queries.shape[-1]
    back_split = back.reshape(queries.shape)
    soft_grad = jnp.einsum("bqhd,bkhd->bhqk", back_split, value_rows, precision=highest)
    value_grad = jnp.einsum("bhqk,bqhd->bkhd", softmaxed, back_split, precision=highest).reshape(
        row_count, feature_width
    )
    score_grad = (
        softmaxed
        * (soft_grad - jnp.sum(soft_grad * softmaxed, axis=-1, keepdims=True))
        / math.sqrt(head_width)
    )
    query_grad = jnp.einsum("bhqk,bkhd->bqhd", score_grad, key_rows, precision=highest).reshape(
        row_count, feature_width
    )
    key_grad = jnp.einsum("bhqk,bqhd->bkhd", score_grad, queries, precision=highest).reshape(
        row_count, feature_width
    )
    hidden_grad = query_grad * query_row + key_grad * key_row + value_grad
    normed_grad = hidden_grad * gain_row
    first_mean = jnp.mean(normed_grad, axis=-1, keepdims=True)
    second_mean = jnp.mean(normed_grad * normed, axis=-1, keepdims=True)
    input_grad = (
        cotangent.astype(jnp.float32) + inverse * (normed_grad - first_mean - normed * second_mean)
    ).astype(jnp.bfloat16)
    sums = jnp.stack(
        [
            jnp.sum(hidden_grad * normed, axis=0),
            jnp.sum(query_grad * hidden, axis=0),
            jnp.sum(key_grad * hidden, axis=0),
        ]
    )
    return (input_grad, sums)


def shards(
    section_inputs,
    norm_gain,
    query_gain,
    key_gain,
    output_weight,
    full_sequence_gradient,
    patch_order,
):
    inputs = section_inputs[0]
    row_count, feature_width = inputs.shape
    image_count = row_count // KEPT
    section = lax.axis_index("section")
    sections = lax.axis_size("section")
    all_images = image_count * lax.axis_size("dp")
    gain_row = norm_gain[0]
    query_row = query_gain[0]
    key_row = key_gain[0]
    weight = gather_rows(output_weight[0])
    normed, inverse = normalize(inputs)
    hidden, queries, key_rows, value_rows, softmaxed, mixed = attend_forward(
        normed, gain_row, query_row, key_row, HEADS
    )
    kept = patch_order[:, :KEPT]
    chosen_patches = (
        kept[:, :, None] == jnp.arange(PATCHES, dtype=jnp.int32)[None, None, :]
    ).astype(jnp.bfloat16)
    upper_bound = (
        jnp.einsum(
            "usn,unj->usj",
            chosen_patches,
            full_sequence_gradient,
            preferred_element_type=jnp.float32,
        )
        .astype(jnp.bfloat16)
        .reshape(row_count, feature_width)
    )
    per_unit = image_count // MICRO
    unit_rows = per_unit * KEPT
    unit_count = image_count // per_unit
    step_count = unit_count + sections - 1

    def take_rows(array, unit):
        return lax.dynamic_slice_in_dim(array, unit * unit_rows, unit_rows, 0)

    def take_images(array, unit):
        return lax.dynamic_slice_in_dim(array, unit * per_unit, per_unit, 0)

    def put_rows(array, piece, unit, valid):
        present_value = take_rows(array, unit)
        return lax.dynamic_update_slice_in_dim(
            array, jnp.where(valid, piece, present_value), unit * unit_rows, 0
        )

    def advance(step_index, carry):
        received, cotangents, input_grads, sums, running_weight = carry
        unit = step_index - (sections - 1 - section)
        valid = jnp.logical_and(unit >= 0, unit < unit_count)
        safe_unit = jnp.clip(unit, 0, unit_count - 1)
        cotangent = jnp.where(section == sections - 1, take_rows(upper_bound, safe_unit), received)
        back = lax.dot_general(
            cotangent, weight, (((1,), (1,)), ((), ())), preferred_element_type=jnp.float32
        )
        input_grad, partial_sums = attend_backward(
            cotangent,
            back,
            take_rows(normed, safe_unit),
            take_rows(inverse, safe_unit),
            take_rows(hidden, safe_unit),
            take_images(queries, safe_unit),
            take_images(key_rows, safe_unit),
            take_images(value_rows, safe_unit),
            take_images(softmaxed, safe_unit),
            gain_row,
            query_row,
            key_row,
        )
        cotangents = put_rows(cotangents, cotangent, safe_unit, valid)
        input_grads = put_rows(input_grads, input_grad, safe_unit, valid)
        sums = sums + jnp.where(valid, partial_sums, 0.0)
        received = from_behind(input_grad, "section", -1)
        return (received, cotangents, input_grads, sums, running_weight)

    weight_offset = jnp.zeros((1,), jnp.float32)
    start_carry = (
        jnp.zeros((unit_rows, feature_width), jnp.bfloat16),
        jnp.zeros_like(inputs),
        jnp.zeros_like(inputs),
        jnp.zeros((3, feature_width), jnp.float32),
        weight_offset,
    )
    final_carry = lax.fori_loop(0, step_count, advance, start_carry)
    cotangents = final_carry[1]
    input_grads = final_carry[2]
    ordered = relative_order(mixed)
    weight_share, gain_total = reduce_rows(
        ordered,
        jnp.pad(cotangents, ((0, 256 - row_count), (0, 0))),
        final_carry[3].reshape(48, 128),
        1.0 / all_images,
    )
    gain_total = gain_total.reshape(3, feature_width)
    return (input_grads[None], weight_share[None], gain_total[None])


def solution(mesh):
    return jax.shard_map(
        shards,
        mesh=mesh,
        in_specs=(
            P("section", "dp", None),
            P("section", None),
            P("section", None),
            P("section", None),
            P("section", "dp", None),
            P("dp", None, None),
            P("dp", None),
        ),
        out_specs=(P("section", "dp", None), P("section", "dp", None), P("section", None, None)),
        check_vma=False,
    )
```
